128 devices in a mesh: seq: 32 (over x, y, core), head: 4 (over z).
Axes of the slice: x: 4, y: 4, z: 4, core: 2. Of those that a mesh axis runs over, the one named last changes fastest.
Arguments:
- inputs: bfloat16 [32768, 1024], P('seq'), may hold values from -12 to 12
- latents: bfloat16 [2048, 1024], replicated, may hold values from -240 to 240
- query_weight: bfloat16 [1024, 1024], P(None, 'head'), may hold values from -1 to 1
- key_weight: bfloat16 [1024, 1024], P(None, 'head'), may hold values from -1 to 1
- value_weight: bfloat16 [1024, 1024], P(None, 'head'), may hold values from -0.1875 to 0.1875
- out_weight: bfloat16 [1024, 1024], P('head'), may hold values from -0.1875 to 0.1875
- prefix_lengths: int32 [2048], replicated, may hold values from 1 to 32768, as said below
- grad_out: bfloat16 [2048, 1024], P('seq', 'head'), may hold values from -6 to 6
Outputs:
- attention_out: bfloat16 [2048, 1024], P('seq', 'head')
- input_grad: bfloat16 [32768, 1024], P(('seq', 'head'))
- latent_grad: bfloat16 [2048, 1024], P('seq', 'head')
- query_weight_grad: float32 [1024, 1024], P('seq', 'head')
- key_weight_grad: float32 [1024, 1024], P('seq', 'head')
- value_weight_grad: float32 [1024, 1024], P('seq', 'head')
- out_weight_grad: float32 [1024, 1024], P('head', 'seq')
The draws below stay inside these ranges and needn't reach their ends.
Inputs may be any that keep to these rules, and one draw needn't show every extreme that they name: `prefix_lengths`: nondecreasing in the latent index; the first is 1 and the last is 32768; all others are 2 or more.
All inputs are finite; a program needn't handle non-finite values.
Results may differ from the reference program's by a relative error of at most 0.012.
Values may be sent and summed in bfloat16 or wider, within the bound.
A program may use at most 128 MiB of HBM per device.

```python
import jax
import jax.numpy as jnp
from jax import lax

D = 1024
H = 16
DH = 64
M = 2048
TOKENS = 32768


def shared_fields(key):
    inputs = jnp.clip(jax.random.normal(jax.random.fold_in(key, 101), (TOKENS, D), jnp.float32), -6.0, 6.0)
    latents = jnp.clip(jax.random.normal(jax.random.fold_in(key, 102), (M, D), jnp.float32), -6.0, 6.0)
    key_weight = jnp.clip(jax.random.normal(jax.random.fold_in(key, 103), (D, H * DH), jnp.float32), -6.0, 6.0) * D ** (-0.5)
    query_weight = jnp.clip(jax.random.normal(jax.random.fold_in(key, 104), (D, H * DH), jnp.float32), -6.0, 6.0) * D ** (-0.5)
    return (inputs, latents, query_weight, key_weight)


def draw_inputs(key, part):
    return shared_fields(key)[0].astype(jnp.bfloat16)


def draw_latents(key, part):
    return shared_fields(key)[1].astype(jnp.bfloat16)


def draw_query_weight(key, part):
    return shared_fields(key)[2].astype(jnp.bfloat16)


def draw_key_weight(key, part):
    return shared_fields(key)[3].astype(jnp.bfloat16)


def draw_prefix_lengths(key, part):
    lengths = jnp.sort(jax.random.randint(jax.random.fold_in(key, 7), (M,), 2, TOKENS + 1, jnp.int32))
    return lengths.at[0].set(1).at[M - 1].set(TOKENS).astype(jnp.int32)


def block_levels(own_key, shape, split, low, top_value):
    def one(axis_at, blocks):
        draws = jax.random.uniform(jax.random.fold_in(jax.random.fold_in(own_key, 6), axis_at), (blocks,), jnp.float32, low / len(split), top_value / len(split))
        return jnp.repeat(jnp.exp(draws), shape[axis_at] // blocks).reshape((-1,) + (1,) * (len(shape) - axis_at - 1))

    level = one(*split[0])
    for cut in split[1:]:
        level = level * one(*cut)
    return level


def gaussian(stream_key, dims, width, most, shards=(), kind=jnp.bfloat16):
    factor_of = block_levels(stream_key, dims, shards, -0.22, 0.18) if shards else 1.0
    values = jax.random.normal(stream_key, dims, jnp.float32) * width * factor_of
    return jnp.minimum(jnp.maximum(values, -most), most).astype(kind)


def setup_inputs(seed: int = 0) -> dict:
    keys = jax.random.split(jax.random.key(seed), 9)
    inputs = draw_inputs(jax.random.fold_in(keys[8], 71), 0)
    latents = draw_latents(jax.random.fold_in(keys[8], 71), 0)
    query_weight = draw_query_weight(jax.random.fold_in(keys[8], 71), 0)
    key_weight = draw_key_weight(jax.random.fold_in(keys[8], 71), 0)
    value_weight = gaussian(keys[4], (D, H * DH), D ** -0.5, 0.1875, ((1, 4),))
    out_weight = gaussian(keys[5], (H * DH, D), (H * DH) ** -0.5, 0.1875, ((0, 4),))
    prefix_lengths = draw_prefix_lengths(jax.random.fold_in(keys[8], 71), 0)
    grad_out = gaussian(keys[7], (M, D), 1.0, 6.0, ((0, 32), (1, 4)))
    return {"inputs": inputs, "latents": latents, "query_weight": query_weight, "key_weight": key_weight, "value_weight": value_weight, "out_weight": out_weight, "prefix_lengths": prefix_lengths, "grad_out": grad_out}


floor_value = -1e30


def widen(array):
    return lax.optimization_barrier(array).astype(jnp.float32)


def reference(inputs, latents, query_weight, key_weight, value_weight, out_weight, prefix_lengths, grad_out):
    scaling = DH ** -0.5
    block_len = min(1024, TOKENS)
    block_total = TOKENS // block_len
    queries = widen(jnp.dot(latents, query_weight, preferred_element_type=jnp.float32).astype(jnp.bfloat16)).reshape(M, H, DH)
    key_rows = widen(jnp.dot(inputs, key_weight, preferred_element_type=jnp.float32).astype(jnp.bfloat16)).reshape(block_total, block_len, H, DH)
    value_rows = widen(jnp.dot(inputs, value_weight, preferred_element_type=jnp.float32).astype(jnp.bfloat16)).reshape(block_total, block_len, H, DH)
    positions = jnp.arange(TOKENS, dtype=jnp.int32).reshape(block_total, block_len)

    def scored(key_block, pos_block):
        scores = jnp.einsum("qhd,khd->hqk", queries, key_block) * scaling
        visible = pos_block[None, None, :] < prefix_lengths[None, :, None]
        return scores, visible

    def max_step(state, blocks):
        key_block, value_block, pos_block = blocks
        scores, visible = scored(key_block, pos_block)
        return jnp.maximum(state, jnp.where(visible, scores, floor_value).max(axis=2)), None

    row_top = lax.scan(max_step, jnp.full((H, M), floor_value, jnp.float32), (key_rows, value_rows, positions))[0]

    def sum_step(state, blocks):
        key_block, value_block, pos_block = blocks
        scores, visible = scored(key_block, pos_block)
        weights = jnp.where(visible, jnp.exp(scores - row_top[:, :, None]), 0.0)
        weighted = jnp.einsum("hqk,khd->qhd", widen(weights.astype(jnp.bfloat16)), value_block)
        return (state[0] + weights.sum(axis=2), state[1] + weighted), None

    start_state = (jnp.zeros((H, M), jnp.float32), jnp.zeros((M, H, DH), jnp.float32))
    exp_total, weighted_sum = lax.scan(sum_step, start_state, (key_rows, value_rows, positions))[0]
    attended = (weighted_sum / exp_total.T[:, :, None]).astype(jnp.bfloat16).reshape(M, H * DH)
    attention_out = jnp.dot(attended, out_weight, preferred_element_type=jnp.float32).astype(jnp.bfloat16)
    dout = jnp.dot(grad_out, out_weight.T, preferred_element_type=jnp.float32).astype(jnp.bfloat16)
    out_weight_grad = jnp.dot(attended.T, grad_out, preferred_element_type=jnp.float32)
    dout_wide = widen(dout).reshape(M, H, DH)
    inner = jnp.sum(dout_wide * widen(attended).reshape(M, H, DH), axis=2).T

    def grad_step(state, blocks):
        key_block, value_block, pos_block = blocks
        scores, visible = scored(key_block, pos_block)
        probs = jnp.where(visible, jnp.exp(scores - row_top[:, :, None]) / exp_total[:, :, None], 0.0)
        dprobs = jnp.einsum("qhd,khd->hqk", dout_wide, value_block)
        dscores = widen((scaling * probs * (dprobs - inner[:, :, None])).astype(jnp.bfloat16))
        new_state = state + jnp.einsum("hqk,khd->qhd", dscores, key_block)
        key_grad = jnp.einsum("hqk,qhd->khd", dscores, queries).astype(jnp.bfloat16)
        value_grad = jnp.einsum("hqk,qhd->khd", widen(probs.astype(jnp.bfloat16)), dout_wide).astype(jnp.bfloat16)
        return new_state, (key_grad, value_grad)

    query_grad, grads = lax.scan(grad_step, jnp.zeros((M, H, DH), jnp.float32), (key_rows, value_rows, positions))
    query_round = query_grad.astype(jnp.bfloat16).reshape(M, H * DH)
    key_grads = grads[0].reshape(TOKENS, H * DH)
    value_grads = grads[1].reshape(TOKENS, H * DH)
    query_weight_grad = jnp.dot(latents.T, query_round, preferred_element_type=jnp.float32)
    latent_grad = jnp.dot(query_round, query_weight.T, preferred_element_type=jnp.float32).astype(jnp.bfloat16)
    key_weight_grad = jnp.dot(inputs.T, key_grads, preferred_element_type=jnp.float32)
    value_weight_grad = jnp.dot(inputs.T, value_grads, preferred_element_type=jnp.float32)
    input_grad = (jnp.dot(key_grads, key_weight.T, preferred_element_type=jnp.float32) + jnp.dot(value_grads, value_weight.T, preferred_element_type=jnp.float32)).astype(jnp.bfloat16)
    return (attention_out, input_grad, latent_grad, query_weight_grad, key_weight_grad, value_weight_grad, out_weight_grad)
```

```python
import functools

import jax
import jax.numpy as jnp
from jax import lax
from jax.experimental import pallas as pl
from jax.experimental.pallas import tpu as pltpu
from jax.sharding import PartitionSpec as P

MESH = pl.DeviceIdType.MESH
F32 = jnp.float32
BF16 = jnp.bfloat16
DH = 64
NS = 32
NC = 16
NZ = 4
NB = 8
QB = 256
KEYS = 1024
CH = 512
FLOOR = -1e30
LOG2E = 1.4426950408889634
(G, W, WF, A, AT, AF, OG, OS, L, SW, ZO, DG, ZK, ZV, LG, RC, RD, OC, SC, DC, A2) = (
    0, 1, 2, 3, 4, 5, 6, 7, 8, 9, 10, 11, 12, 13, 14, 15, 19, 24, 25, 26, 23)
NT = (((1,), (1,)), ((), ()))
TN = (((0,), (0,)), ((), ()))


def dotf(a, b, dims=None):
    if dims is None:
        return jnp.dot(a, b, preferred_element_type=F32)
    return lax.dot_general(a, b, dims, preferred_element_type=F32)


def each(low, high, body):
    def step(i, carry):
        body(i)
        return carry

    lax.fori_loop(low, high, step, 0)


def rows(i, n):
    return pl.ds(pl.multiple_of(i * n, n), n)


def mixed(pair, other, half):
    lane = lax.broadcasted_iota(jnp.int32, pair.shape, 1)
    keep = (lane < DH) if half == 0 else (lane >= DH)
    return jnp.where(keep, pair, other)


def split(value):
    high = value.astype(BF16).astype(F32)
    return jnp.concatenate([high, value - high], axis=0).astype(BF16)


def doubled(pair, half):
    return mixed(pair, pltpu.roll(pair, DH, 1), half).astype(BF16)


def half_mask(value, half):
    return mixed(value, jnp.zeros_like(value), half)


def shifted(me, d):
    x = (me // 8 + d // 8) % 4
    y = (me // 2 + d // 2) % 4
    return (x * 4 + y) * 2 + (me + d) % 2


def chip_ahead(chip, e):
    return ((chip // 4 + e // 4) % 4) * 4 + (chip + e) % 4


def chip_behind(chip, e):
    return ((chip // 4 + 4 - e // 4) % 4) * 4 + (chip + 16 - e) % 4


def offset_to(chip, target):
    return ((target // 4 + 4 - chip // 4) % 4) * 4 + (target + 16 - chip) % 4


def take(ref, sem):
    pltpu.make_async_copy(ref, ref, sem).wait()


def to_seq(src, dst, send, recv, j):
    return pltpu.make_async_remote_copy(
        src_ref=src, dst_ref=dst, send_sem=send, recv_sem=recv, device_id={"seq": j}, device_id_type=MESH)


def to_head(src, dst, send, recv, j):
    return pltpu.make_async_remote_copy(
        src_ref=src, dst_ref=dst, send_sem=send, recv_sem=recv, device_id={"head": j}, device_id_type=MESH)


def layer_kernel(
    x_h, lat_h, wq_h, wk_h, wv_h, wo_h, g_ref, pref_ref,
    ao_ref, ig_ref, lg_ref, dwq_ref, dwk_ref, dwv_ref, dwo_ref,
    x_v, lat_v, wq_v, w_all, wo_v, g4, q_v, qt_v, kz, vz, vt, kt, da_v, e_v, s_buf,
    ot_v, st_v, oc_v, sc_v, pre_v, prs_v, og_v, ogs_v, lrb, lrs, lr_v, att_v, att_s, aop, aor,
    dq_v, dqc, dqs, dqr, dqt, dkt, dsbuf, das, dav, sh_v, dq0, dv_acc, dk_v, dv_v, zk, zv, rp, rc, rs, rg, lgp, lgr,
    ld, snd, rcv, oc_r, sc_r, dc_r,
):
    me = lax.axis_index("seq")
    z = lax.axis_index("head")
    core = me % 2
    chip = me // 2
    twin = me + 1 - 2 * core
    base = me * KEYS

    def turn(i):
        near = i + 1
        mixed_up = jnp.where(i < 6, i + 2 - 2 * (i % 2), near)
        step = jnp.where(chip % 2 == 0, near, 32 - mixed_up)
        return (chip // 2 + step) % NB

    loads = [
        pltpu.make_async_copy(wk_h, w_all.at[0, z], ld.at[0]),
        pltpu.make_async_copy(wq_h, wq_v, ld.at[1]),
        pltpu.make_async_copy(lat_h, lat_v, ld.at[2]),
        pltpu.make_async_copy(wo_h, wo_v, ld.at[3]),
        pltpu.make_async_copy(wv_h, w_all.at[1, z], ld.at[4]),
    ]
    loads[0].start()
    for part in range(2):
        for r in range(4):
            pltpu.make_async_copy(
                x_h.at[r * 256 + part * 128:r * 256 + part * 128 + 128, :],
                x_v.at[part * CH + r * 128:part * CH + r * 128 + 128, :], ld.at[5]).start()
    for load in loads[1:]:
        load.start()
    barrier = pltpu.get_barrier_semaphore()

    @functools.partial(each, 1, NS)
    def _(d):
        pl.semaphore_signal(barrier, inc=1, device_id={"seq": shifted(me, d)}, device_id_type=MESH)

    for dz in range(1, NZ):
        pl.semaphore_signal(barrier, inc=1, device_id={"head": (z + dz) % NZ}, device_id_type=MESH)

    g4[z] = g_ref[...]
    row16 = lax.broadcasted_iota(jnp.int32, (16, KEYS), 0)
    ones = jnp.where(row16 == 0, 1.0, 0.0).astype(BF16)
    for h in range(4):
        vt[h, 64:80, :] = ones
    for p in range(2):
        for t in range(NC):
            st_v[p, t, 4:8, :] = jnp.zeros((4, 128), F32)
    loads[0].wait()
    take(x_v, ld.at[5])

    @functools.partial(each, 0, 2)
    def _(i):
        for j in range(2):
            at = rows(2 * i + j, 256)
            block = dotf(x_v[at, :], w_all[0, z]).astype(BF16).astype(F32)
            kt[:, at] = block.T.astype(BF16)
            for h in range(4):
                kz[h, at, :] = doubled(block[:, (h // 2) * 128:(h // 2) * 128 + 128], h % 2)

    loads[4].wait()

    @functools.partial(each, 0, 2)
    def _(i):
        for j in range(2):
            at = rows(2 * i + j, 256)
            block = dotf(x_v[at, :], w_all[1, z]).astype(BF16).astype(F32)
            flipped = block.T.astype(BF16)
            for h in range(4):
                vz[h, at, :] = doubled(block[:, (h // 2) * 128:(h // 2) * 128 + 128], h % 2)
                vt[h, 0:64, at] = flipped[h * 64:(h + 1) * 64, :]

    loads[1].wait()
    loads[2].wait()

    @functools.partial(each, 0, NB // 2)
    def _(i):
        for j in range(2):
            at = rows(2 * i + j, 256)
            block = (dotf(lat_v[at, :], wq_v[...]).astype(BF16).astype(F32) * 0.125)
            flipped = block.T
            qt_v[:, at] = flipped.astype(BF16)
            flipped = flipped * LOG2E
            for h in range(4):
                q_v[h, :, at] = split(flipped[h * 64:h * 64 + 64, :])

    pl.semaphore_wait(barrier, NS - 1 + NZ - 1)

    def g_copy(dz):
        return to_head(g_ref, g4.at[z], snd.at[G], rcv.at[G], (z + dz) % NZ)

    def w_copy(dz):
        return to_head(w_all.at[core, z], w_all.at[core, z], snd.at[W], rcv.at[W], (z + dz) % NZ)

    def wf_copy(dz):
        src = (z + NZ - dz) % NZ
        return to_seq(w_all.at[core, src], w_all.at[core, src], snd.at[WF], rcv.at[WF], twin)

    for dz in range(1, NZ):
        g_copy(dz).start()

    own_da = da_v.at[rows(me, 64), :]

    def a_first(k):
        t = chip_ahead(chip, jnp.where(core == 0, 4 * k, k))
        return to_seq(own_da, own_da, snd.at[A], rcv.at[A], 2 * t + core)

    def a_second(k, j):
        piece = da_v.at[rows(2 * chip_behind(chip, jnp.where(core == 0, 4 * j, j)) + core, 64), :]
        t = chip_ahead(chip, jnp.where(core == 0, k, 4 * k))
        return to_seq(piece, piece, snd.at[A2], rcv.at[A2], 2 * t + core)

    def a_twin():
        return to_seq(own_da, own_da, snd.at[AT], rcv.at[AT], twin)

    def af_copy(e):
        piece = da_v.at[rows(2 * chip_behind(chip, e) + core, 64), :]
        return to_seq(piece, piece, snd.at[AF], rcv.at[AF], twin)

    def own_cotangent():
        loads[3].wait()
        take(g4.at[0:3], rcv.at[G])
        acc = dotf(g4[0], wo_v[:, 0:256], NT)
        for i in range(1, NZ):
            acc = acc + dotf(g4[i], wo_v[:, i * 256:(i + 1) * 256], NT)
        da_v[rows(me, 64), :] = acc.astype(BF16)

    def send_cotangent():
        a_twin().start()

        for k in range(1, 4):
            a_first(k).start()

        for dz in range(1, NZ):
            w_copy(dz).start()

    def scores(b, h, slot, c):
        s = dotf(kz[h, c * CH:c * CH + CH, :], q_v[h, :, rows(b, QB)])
        pos = lax.broadcasted_iota(jnp.int32, (128, QB), 0)
        left = pref_ref[:, rows(b, QB)] - base - c * 128
        top = None
        for r in range(4):
            part = jnp.where(pos < left - r * 256, s[r * 128:r * 128 + 128, :], FLOOR)
            s_buf[slot, c * CH + r * 128:c * CH + r * 128 + 128, :] = part
            best = jnp.max(part, axis=0, keepdims=True)
            top = best if r == 0 else jnp.maximum(top, best)
        return top

    def oc_copy(b):
        pair = pl.ds(2 * b, 2)
        return to_seq(ot_v.at[1 - core, pair], oc_v.at[pair], snd.at[OC], oc_r.at[b], twin)

    def sc_copy(b):
        pair = pl.ds(2 * b, 2)
        return to_seq(st_v.at[1 - core, pair], sc_v.at[pair], snd.at[SC], sc_r.at[b], twin)

    def og_copy(t, e):
        return to_seq(pre_v.at[t], og_v.at[e], snd.at[OG], rcv.at[OG], 2 * t + core)

    def os_copy(t, e):
        return to_seq(prs_v.at[t], ogs_v.at[e], snd.at[OS], rcv.at[OS], 2 * t + core)

    def merge_out(b):
        oc_copy(b).wait_recv()
        sc_copy(b).wait_recv()
        for sub in range(2):
            t = 2 * b + sub
            mine = st_v[core, t]
            other = sc_v[t]
            top = jnp.maximum(mine, other)
            wa = jnp.exp2(mine - top)
            wb = jnp.exp2(other - top)
            prs_v[t, 0:2, :] = top[0:2, :]
            prs_v[t, 2:4, :] = wa[0:2, :] * mine[2:4, :] + wb[0:2, :] * other[2:4, :]
            prs_v[t, 4:8, :] = jnp.zeros((4, 128), F32)
            for half in range(2):
                cut = slice(half * 64, half * 64 + 64)
                pre_v[t, cut, :] = wa[half:half + 1, :] * ot_v[core, t, cut, :] + wb[half:half + 1, :] * oc_v[t, cut, :]
        for sub in range(2):
            t = 2 * b + sub
            e = offset_to(chip, t)

            @pl.when(e != 0)
            def _():
                og_copy(t, e).start()
                os_copy(t, e).start()

            @pl.when(e == 0)
            def _():
                og_v[0] = pre_v[t]
                ogs_v[0] = prs_v[t]

    def forward_block(i, m):
        b = turn(i)
        following = turn(i + 1)
        for h in range(4):
            p, half = h // 2, h % 2
            oz = None
            m_next = None
            for c in range(KEYS // CH):
                at = slice(c * CH, c * CH + CH)
                if h < 3:
                    part = scores(b, h + 1, (h + 1) % 2, c)
                else:
                    part = scores(following, 0, 0, c)
                m_next = part if c == 0 else jnp.maximum(m_next, part)
                e = jnp.exp2(s_buf[h % 2, at, :] - m).astype(BF16)
                e_v[b * 2 + p, at, half * QB:half * QB + QB] = e
                term = dotf(vt[h, :, at], e)
                oz = term if c == 0 else oz + term
            for sub in range(2):
                cut = slice(sub * 128, sub * 128 + 128)
                ot_v[p, 2 * b + sub, half * 64:half * 64 + 64, :] = oz[0:64, cut]
                st_v[p, 2 * b + sub, half:half + 1, :] = m[:, cut]
                st_v[p, 2 * b + sub, 2 + half:3 + half, :] = oz[64:65, cut]
            m = m_next
        oc_copy(b).start()
        sc_copy(b).start()

        @pl.when(i > 1)
        def _():
            merge_out(turn(i - 2))

        @pl.when(i == 4)
        def _():
            own_cotangent()

        @pl.when(i == 5)
        def _():
            send_cotangent()

        @pl.when(i == 7)
        def _():
            take(da_v.at[0:192, :], rcv.at[A])

            @functools.partial(each, 0, 4)
            def _(j):
                for k in range(1, 4):
                    a_second(k, j).start()

        return m

    start = None
    for c in range(KEYS // CH):
        part = scores(turn(0), 0, 0, c)
        start = part if c == 0 else jnp.maximum(start, part)
    lax.fori_loop(0, NB, forward_block, start)
    merge_out(turn(NB - 2))
    merge_out(turn(NB - 1))

    take(da_v.at[0:64, :], rcv.at[AT])
    take(og_v.at[1:NC], rcv.at[OG])
    take(ogs_v.at[1:NC], rcv.at[OS])
    stats = ogs_v[...]
    top = jnp.max(stats, axis=0, keepdims=True)
    weight = jnp.exp2(stats - top)
    sums = jnp.concatenate([stats[:, 2:8, :], stats[:, 0:2, :]], axis=1)
    total = jnp.sum(weight * sums, axis=0, keepdims=True)
    level = top[0] + jnp.log(total[0]) * LOG2E
    coef = weight / total
    halves = []
    for half in range(2):
        acc = jnp.zeros((64, 128), F32)
        for j in range(NC):
            acc = acc + coef[j, half:half + 1, :] * og_v[j, half * 64:half * 64 + 64, :]
        halves.append(acc.astype(BF16).astype(F32))
    attended_t = jnp.concatenate(halves, axis=0)
    da_t = da_v[rows(chip, 128), rows(core, 128)].astype(F32).T
    prod = da_t * attended_t
    lrs[0:2, :] = level[0:2, :]
    lrs[2:3, :] = jnp.sum(prod[0:64, :], axis=0, keepdims=True)
    lrs[3:4, :] = jnp.sum(prod[64:128, :], axis=0, keepdims=True)
    lrs[4:8, :] = jnp.zeros((4, 128), F32)
    lrb[me] = lrs[...]
    att_s[...] = attended_t.T.astype(BF16)

    def l_copy(d):
        return to_seq(lrs, lrb.at[me], snd.at[L], rcv.at[L], shifted(me, d))

    def at_copy():
        return to_seq(att_s.at[rows(1 - core, 64), :], att_v.at[core], snd.at[SW], rcv.at[SW], twin)

    for d in range(1, NS):
        l_copy(d).start()

    take(da_v.at[0:768, :], rcv.at[A2])

    for e in range(1, NC):
        af_copy(e).start()

    at_copy().start()
    att_v[core] = att_s[rows(core, 64), :]
    take(att_v.at[0], rcv.at[SW])
    attended = jnp.concatenate([att_v[0], att_v[1]], axis=1)
    for i in range(NZ):
        aop[i] = dotf(attended, wo_v[:, i * 256:(i + 1) * 256]).astype(BF16)
    for i in range(NZ):
        rp[0, 4 * i:4 * i + 4] = dotf(g4[i], attended, TN).astype(BF16).reshape(4, 2, 32, 256)

    def zo_copy(dz):
        t = (z + dz) % NZ
        return to_head(aop.at[t], aor.at[dz], snd.at[ZO], rcv.at[ZO], t)

    for dz in range(1, NZ):
        zo_copy(dz).start()

    def rc_copy(n):
        return to_seq(rp.at[n, :, 1 - core], rc.at[n], snd.at[RC + n], rcv.at[RC + n], twin)

    def rd_copy(n, e):
        t = chip_ahead(chip, e)
        return to_seq(rs.at[n, t], rg.at[n, e], snd.at[RD + n], rcv.at[RD + n], 2 * t + core)

    def reduce_mid(n):
        take(rc.at[n], rcv.at[RC + n])
        rs[n] = (rp[n, :, core].astype(F32) + rc[n].astype(F32)).astype(BF16)
        rg[n, 0] = rs[n, chip]

        for e in range(1, NC):
            rd_copy(n, e).start()

    def reduce_end(n):
        take(rg.at[n, 1:NC], rcv.at[RD + n])
        grad = rg[n, 0].astype(F32)
        for e in range(1, NC):
            grad = grad + rg[n, e].astype(F32)
        return grad

    rc_copy(0).start()
    dkt[...] = jnp.zeros_like(dkt)
    take(da_v.at[0:960, :], rcv.at[AF])
    take(lrb.at[0:NS - 1], rcv.at[L])
    for t in range(NC):
        lr_v[0:4, t * 128:(t + 1) * 128] = lrb[2 * t, 0:4, :]
        lr_v[4:8, t * 128:(t + 1) * 128] = lrb[2 * t + 1, 0:4, :]

    def dc_copy(b):
        pair = pl.ds(2 * b, 2)
        return to_seq(dq_v.at[pair, 1 - core], dqc.at[pair], snd.at[DC], dc_r.at[b], twin)

    def dg_copy(t, e):
        return to_seq(dqs.at[t], dqr.at[e], snd.at[DG], rcv.at[DG], 2 * t + core)

    def merge_dq(b):
        dc_copy(b).wait_recv()
        for sub in range(2):
            t = 2 * b + sub
            dqs[t] = (dq_v[t, core].astype(F32) + dqc[t].astype(F32)).astype(BF16)
        for sub in range(2):
            t = 2 * b + sub
            e = offset_to(chip, t)

            @pl.when(e != 0)
            def _():
                dg_copy(t, e).start()

            @pl.when(e == 0)
            def _():
                dqr[0] = dqs[t]

    @functools.partial(each, 0, NB)
    def _(b):
        at = rows(b, QB)
        da_t = da_v[at, :].astype(F32).T
        scaled = []
        for h in range(4):
            p, half = h // 2, h % 2
            local = jnp.concatenate([st_v[p, 2 * b], st_v[p, 2 * b + 1]], axis=1)[half:half + 1, :]
            factor = jnp.exp2(local - lr_v[4 * p + half:4 * p + half + 1, at])
            part = da_t[h * 64:h * 64 + 64, :] * factor
            das[h, :, at] = split(part)
            scaled.append(part)
            sh_v[h:h + 1, at] = lr_v[4 * p + 2 + half:4 * p + 3 + half, at] * factor
        da_s = jnp.concatenate(scaled, axis=0).T
        for p in range(2):
            pair = da_s[:, p * 128:(p + 1) * 128]
            for half in range(2):
                dav[p, rows(2 * b + half, QB), :] = half_mask(pair, half).astype(BF16)

    dv_acc[...] = jnp.zeros_like(dv_acc)

    def weight_term(n, grad_ref):
        @functools.partial(each, 0, 4)
        def _(i):
            term = dotf(x_v[:, rows(i, 256)], grad_ref[...], TN)
            rp[n, rows(i, 4)] = term.astype(BF16).reshape(4, 2, 32, 256)

        rc_copy(n).start()

    def cotangent(part, b, h):
        p, half = h // 2, h % 2
        span = slice(part * CH, part * CH + CH)
        at = rows(b, QB)
        dprob = (dotf(vz[h, span, :], das[h, :, at]) - sh_v[h:h + 1, at]).astype(BF16)
        dsbuf[half] = e_v[b * 2 + p, span, half * QB:half * QB + QB] * dprob

    def backward_block(part, i):
        b = turn(i)
        following = turn(i + 1)
        at = rows(b, QB)
        span = slice(part * CH, part * CH + CH)
        for h in range(4):
            cut = slice(h * 64, h * 64 + 64)
            p, half = h // 2, h % 2
            if h < 3:
                cotangent(part, b, h + 1)
            else:
                cotangent(part, following, 0)
            grad = dotf(kt[cut, span], dsbuf[half])
            if part == 0:
                dq0[b, cut, :] = grad
            else:
                dqt[cut, :] = dq0[b, cut, :] + grad
            dkt[cut, span] += dotf(qt_v[cut, at], dsbuf[half], NT)
            piece = slice(part * CH + half * (CH // 2), part * CH + (half + 1) * (CH // 2))
            dv_acc[piece, p * 128:(p + 1) * 128] += dotf(e_v[b * 2 + p, piece, :], dav[p, rows(b, 2 * QB), :])

    def zk_copy(part, dz):
        t = (z + dz) % NZ
        return to_head(dk_v.at[pl.ds(pl.multiple_of(part * CH + t * 128, 128), 128), :],
                       zk.at[dz, part * 128:part * 128 + 128], snd.at[ZK], rcv.at[ZK], t)

    def zv_copy(part, dz):
        t = (z + dz) % NZ
        return to_head(dv_v.at[pl.ds(pl.multiple_of(part * CH + t * 128, 128), 128), :],
                       zv.at[dz, part * 128:part * 128 + 128], snd.at[ZV], rcv.at[ZV], t)

    def half_done(part):
        span = slice(part * CH, part * CH + CH)
        dv_v[span, :] = dv_acc[span, :].astype(BF16)
        dk_v[span, :] = dkt[:, span].T.astype(BF16)
        own = pl.ds(pl.multiple_of(part * CH + z * 128, 128), 128)
        zk[0, part * 128:part * 128 + 128, :] = dk_v[own, :]
        zv[0, part * 128:part * 128 + 128, :] = dv_v[own, :]
        for dz in (2, 1, 3):
            zv_copy(part, dz).start()
            zk_copy(part, dz).start()

    cotangent(0, turn(0), 0)

    @functools.partial(each, 0, NB // 2)
    def _(i):
        backward_block(0, 2 * i)
        backward_block(0, 2 * i + 1)

        @pl.when(i == 0)
        def _():
            reduce_mid(0)

    half_done(0)
    cotangent(1, turn(0), 0)

    @functools.partial(each, 0, NB)
    def _(i):
        backward_block(1, i)
        b = turn(i)
        dq_v[pl.ds(2 * b, 2)] = (dqt[...].T * 0.125).astype(BF16).reshape(2, 2, 64, 256)
        dc_copy(b).start()

        @pl.when(i > 1)
        def _():
            merge_dq(turn(i - 2))

        @pl.when(i == 2)
        def _():
            take(w_all.at[0, 0:3], rcv.at[W])
            for dz in range(1, NZ):
                wf_copy(dz).start()

    half_done(1)
    merge_dq(turn(NB - 2))
    weight_term(1, dk_v)
    merge_dq(turn(NB - 1))
    weight_term(2, dv_v)
    reduce_mid(1)
    take(dqr.at[1:NC], rcv.at[DG])

    total = dqr[0].astype(F32)
    for e in range(1, NC):
        total = total + dqr[e].astype(F32)
    dq = total.astype(BF16)
    latents = lat_v[rows(me, 64), :]
    for i in range(4):
        term = dotf(latents[:, i * 256:(i + 1) * 256], dq, TN)
        rp[3, 4 * i:4 * i + 4] = term.astype(BF16).reshape(4, 2, 32, 256)
    rc_copy(3).start()
    for i in range(NZ):
        lgp[i] = dotf(dq, wq_v[i * 256:(i + 1) * 256, :], NT).astype(BF16)

    def lg_copy(dz):
        t = (z + dz) % NZ
        return to_head(lgp.at[t], lgr.at[dz], snd.at[LG], rcv.at[LG], t)

    for dz in range(1, NZ):
        lg_copy(dz).start()
    reduce_mid(2)
    reduce_mid(3)

    take(w_all.at[0, 0:3], rcv.at[WF])
    dwo_ref[...] = reduce_end(0)
    out = aop[z].astype(F32)
    take(aor.at[1:NZ], rcv.at[ZO])
    for dz in range(1, NZ):
        out = out + aor[dz].astype(F32)
    ao_ref[...] = out.astype(BF16)
    dwk_ref[...] = reduce_end(1)
    take(zv.at[1:NZ], rcv.at[ZV])
    take(zk.at[1:NZ], rcv.at[ZK])

    @functools.partial(each, 0, 4)
    def _(i):
        at = rows(i, 256)
        acc = jnp.zeros((256, 256), F32)
        for dz in range(NZ):
            src = (z + NZ - dz) % NZ
            acc = acc + dotf(zk[dz], w_all[0, src, at, :], NT) + dotf(zv[dz], w_all[1, src, at, :], NT)
        ig_ref[:, at] = acc.astype(BF16)

    grad = lgp[z].astype(F32)
    take(lgr.at[1:NZ], rcv.at[LG])
    for dz in range(1, NZ):
        grad = grad + lgr[dz].astype(F32)
    lg_ref[...] = grad.astype(BF16)
    dwv_ref[...] = reduce_end(2)
    dwq_ref[...] = reduce_end(3)

    take(g4.at[0:3], snd.at[G])
    take(w_all.at[0, 0:3], snd.at[W])
    take(w_all.at[0, 0:3], snd.at[WF])
    take(da_v.at[0:192, :], snd.at[A])
    take(da_v.at[0:768, :], snd.at[A2])
    take(da_v.at[0:64, :], snd.at[AT])
    take(da_v.at[0:960, :], snd.at[AF])
    take(og_v.at[1:NC], snd.at[OG])
    take(ogs_v.at[1:NC], snd.at[OS])
    take(lrb.at[0:NS - 1], snd.at[L])
    take(att_v.at[0], snd.at[SW])
    take(aor.at[1:NZ], snd.at[ZO])
    take(dqr.at[1:NC], snd.at[DG])
    take(zk.at[1:NZ], snd.at[ZK])
    take(zv.at[1:NZ], snd.at[ZV])
    take(lgr.at[1:NZ], snd.at[LG])
    take(oc_v, snd.at[OC])
    take(sc_v, snd.at[SC])
    take(dqc, snd.at[DC])
    for n in range(4):
        take(rc.at[n], snd.at[RC + n])
        take(rg.at[n, 1:NC], snd.at[RD + n])


def vspec():
    return pl.BlockSpec(memory_space=pltpu.VMEM)


def hspec():
    return pl.BlockSpec(memory_space=pl.ANY)


OUTS = (
    ((64, 256), BF16), ((256, 1024), BF16), ((64, 256), BF16),
    ((32, 256), F32), ((32, 256), F32), ((32, 256), F32), ((32, 256), F32),
)


def layer(x, lat, wq, wk, wv, wo, g, pref):
    sem = lambda *n: pltpu.SemaphoreType.DMA(n)
    b16 = lambda *n: pltpu.VMEM(n, BF16)
    f32 = lambda *n: pltpu.VMEM(n, F32)
    return pl.pallas_call(
        layer_kernel,
        name="layer",
        out_shape=tuple(jax.ShapeDtypeStruct(s, t) for s, t in OUTS),
        in_specs=[hspec()] * 6 + [vspec()] * 2,
        out_specs=tuple([vspec()] * 7),
        scratch_shapes=[
            b16(1024, 1024), b16(2048, 1024), b16(1024, 256), b16(2, NZ, 1024, 256), b16(256, 1024), b16(NZ, 64, 256),
            b16(4, 128, 2048), b16(256, 2048), b16(4, KEYS, 128), b16(4, KEYS, 128), b16(4, 80, KEYS), b16(256, KEYS),
            b16(2048, 256), b16(16, KEYS, 2 * QB), f32(2, KEYS, QB),
            f32(2, NC, 128, 128), f32(2, NC, 8, 128), f32(NC, 128, 128), f32(NC, 8, 128),
            f32(NC, 128, 128), f32(NC, 8, 128), f32(NC, 128, 128), f32(NC, 8, 128),
            f32(NS, 8, 128), f32(8, 128), f32(8, 2048), b16(2, 64, 128), b16(128, 128), b16(NZ, 64, 256), b16(NZ, 64, 256),
            b16(NC, 2, 64, 256), b16(NC, 64, 256), b16(NC, 64, 256), b16(NC, 64, 256),
            f32(256, QB), f32(256, KEYS), b16(2, CH, QB), b16(4, 128, 2048), b16(2, 4096, 128), f32(8, 2048), f32(NB, 256, QB), f32(KEYS, 256),
            b16(KEYS, 256), b16(KEYS, 256), b16(NZ, 256, 256), b16(NZ, 256, 256),
            b16(4, NC, 2, 32, 256), b16(4, NC, 32, 256), b16(4, NC, 32, 256), b16(4, NC, 32, 256),
            b16(NZ, 64, 256), b16(NZ, 64, 256),
            sem(6), sem(27), sem(24), sem(8), sem(8), sem(8),
        ],
        compiler_params=pltpu.CompilerParams(
            collective_id=0, has_side_effects=True, vmem_limit_bytes=66_000_000),
    )(x, lat, wq, wk, wv, wo, g, pref.reshape(1, 2048))


def finish_kernel(*refs):
    for i in range(7):
        refs[7 + i][...] = refs[i][...]


def finish(parts):
    return pl.pallas_call(
        finish_kernel,
        name="finish",
        out_shape=tuple(jax.ShapeDtypeStruct(s, t) for s, t in OUTS),
        in_specs=[vspec()] * 7,
        out_specs=tuple([vspec()] * 7),
    )(*parts)


def on_device(x, lat, wq, wk, wv, wo, pref, g):
    outs = finish(layer(x, lat, wq, wk, wv, wo, g, pref))
    return outs[:6] + (outs[6].T,)


def solution(mesh):
    return jax.shard_map(
        on_device,
        mesh=mesh,
        in_specs=(
            P("seq", None), P(), P(None, "head"), P(None, "head"), P(None, "head"), P("head", None), P(), P("seq", "head"),
        ),
        out_specs=(
            P("seq", "head"), P(("seq", "head"), None), P("seq", "head"), P("seq", "head"),
            P("seq", "head"), P("seq", "head"), P("head", "seq"),
        ),
        check_vma=False,
    )
```
